32 devices in a mesh: gz: 4 (over z), gy: 8 (over y, x, core).
Axes of the slice: x: 2, y: 2, z: 4, core: 2. Of those that a mesh axis runs over, the one named last changes fastest.
Arguments:
- vel_pre: float32 [3, 192, 1024, 128], P(None, 'gz', 'gy')
- vel_farm: float32 [3, 192, 1024, 384], P(None, 'gz', 'gy')
- thrust: float32 [8], replicated, may hold values from 1 to 4
- turbine_cells: int32 [3, 8, 64], replicated, may hold values from 0 to 1023, as said below
- inflow_rows: int32 [1024], P('gy'), may hold values from 0 to 1023
Outputs:
- new_pre: float32 [3, 192, 1024, 128], P(None, 'gz', 'gy')
- new_farm: float32 [3, 192, 1024, 384], P(None, 'gz', 'gy')
The draws below stay inside these ranges and needn't reach their ends.
Inputs may be any that keep to these rules, and one draw needn't show every extreme that they name: turbine_cells[0], [1], [2] hold z, y, x; the 64 cells of turbine t are z0 + i, y0 + j (0 <= i, j < 8) at one x; the turbines stand in four streamwise rows, several turbines may share a row.
All inputs are finite; a program needn't handle non-finite values.
Results may differ from the reference program's by a relative error of at most 0.0003.
Values sent between devices are 32-bit elements; how exact they have to be, the bound alone decides.
A program may use at most 640 MiB of HBM per device.

```python
import math
import jax
import jax.numpy as jnp
from jax import lax

NY = 1024
NZ = 192
NXP = 128
NXF = 384
FRINGE = 32
NTURB = 8
SIDE = 8


def coherent_wave(key, count, amp_lo, amp_hi):
    key_amp = jax.random.fold_in(key, 1)
    key_phase = jax.random.fold_in(key, 2)
    amplitude = jax.random.uniform(key_amp, (), jnp.float32, amp_lo, amp_hi)
    offset = jax.random.uniform(key_phase, (), jnp.float32, -jnp.pi, jnp.pi)
    places = jnp.arange(count, dtype=jnp.int32)
    phases = count // 6 * places % count
    angles = 2.0 * jnp.pi * phases.astype(jnp.float32) / count
    return amplitude * jnp.sin(angles + offset)


def velocity_field(key, shape):
    depth = shape[1]
    span_count = shape[2]
    stream_count = shape[3]
    heights = (jnp.arange(depth, dtype=jnp.float32) + 0.5) / depth
    noise = jax.random.normal(key, shape, jnp.float32)
    profile = 2.0 * jnp.sqrt(heights)
    noise = noise.at[0].add(profile[:, None, None])
    wave_stream = coherent_wave(jax.random.fold_in(key, 29), stream_count, 5.0, 7.0)
    wave_span = coherent_wave(jax.random.fold_in(key, 31), span_count, 5.0, 7.0)
    noise = noise.at[0].add(wave_stream[None, None, :])
    noise = noise.at[1].add(wave_span[None, :, None])
    return noise


def draw_vel_pre(key, part):
    return velocity_field(jax.random.fold_in(key, 3), (3, NZ, NY, NXP))


def draw_vel_farm(key, part):
    return velocity_field(jax.random.fold_in(key, 5), (3, NZ, NY, 3 * NXP))


def draw_turbine_cells(key, part):
    key_x = jax.random.fold_in(key, 11)
    key_y = jax.random.fold_in(key, 13)
    key_z = jax.random.fold_in(key, 17)
    spacing = 3 * NXP // 4
    row_ids = jnp.arange(4, dtype=jnp.int32)
    jitter = jax.random.randint(key_x, (4,), 0, 8, dtype=jnp.int32)
    jitter = jnp.where(row_ids == 0, 0, jitter)
    row_x = 3 * NXP - 1 - row_ids * spacing - jitter
    turbine_ids = jnp.arange(NTURB, dtype=jnp.int32)
    column = row_x[turbine_ids % 4]
    corner_y = jax.random.randint(key_y, (NTURB,), 0, NY - SIDE + 1, dtype=jnp.int32)
    corner_y = corner_y.at[0].set(NY - SIDE)
    corner_z = jax.random.randint(key_z, (NTURB,), 0, NZ - SIDE + 1, dtype=jnp.int32)
    corner_z = corner_z.at[0].set(0)
    offsets = jnp.arange(SIDE * SIDE, dtype=jnp.int32)
    cell_z = corner_z[:, None] + offsets[None, :] // SIDE
    cell_y = corner_y[:, None] + offsets[None, :] % SIDE
    cell_x = jnp.broadcast_to(column[:, None], cell_z.shape)
    return jnp.stack([cell_z, cell_y, cell_x]).astype(jnp.int32)


def touch_ends(entries, own_key, low, high):
    place = [jax.random.randint(jax.random.fold_in(own_key, axis), (), 0, length) for axis, length in enumerate(entries.shape)]
    widest = entries.shape.index(max(entries.shape))
    beside = place[:widest] + [(place[widest] + 1) % entries.shape[widest]] + place[widest + 1:]
    return entries.at[tuple(place)].set(low).at[tuple(beside)].set(high)


def setup_inputs(seed: int = 0) -> dict:
    key_of = jax.random.split(jax.random.key(seed), 6)
    return {
        "vel_pre": draw_vel_pre(jax.random.fold_in(key_of[5], 71), 0),
        "vel_farm": draw_vel_farm(jax.random.fold_in(key_of[5], 71), 0),
        "thrust": jnp.clip(jnp.exp(jax.random.uniform(key_of[2], (NTURB,), jnp.float32, math.log(1.0), math.log(4.0))), 1.0, 4.0),
        "turbine_cells": draw_turbine_cells(jax.random.fold_in(key_of[5], 71), 0),
        "inflow_rows": touch_ends(jax.random.randint(key_of[4], (NY,), 0, NY), jax.random.fold_in(key_of[4], 1), 0, NY - 1).astype(jnp.int32),
    }


time_step = 0.1
viscosity = 0.05
smagorinsky = 0.03

def tendency(velocity, up_x, dn_x, up_y, dn_y, up_z, dn_z):
    grad_x = 0.5 * (up_x - dn_x)
    grad_y = 0.5 * (up_y - dn_y)
    grad_z = 0.5 * (up_z - dn_z)
    laplace = up_x + dn_x + up_y + dn_y + up_z + dn_z - 6.0 * velocity
    advect = velocity[0:1] * grad_x + velocity[1:2] * grad_y + velocity[2:3] * grad_z
    shear_sq = 2.0 * (grad_x[0] * grad_x[0] + grad_y[1] * grad_y[1] + grad_z[2] * grad_z[2])
    shear_sq = shear_sq + (grad_y[0] + grad_x[1]) * (grad_y[0] + grad_x[1])
    shear_sq = shear_sq + (grad_z[0] + grad_x[2]) * (grad_z[0] + grad_x[2])
    shear_sq = shear_sq + (grad_z[1] + grad_y[2]) * (grad_z[1] + grad_y[2])
    eddy_visc = viscosity + smagorinsky * jnp.sqrt(shear_sq)
    return velocity + time_step * (eddy_visc * laplace - advect)

def predict_domain(velocity):
    depth = velocity.shape[1]
    padded = jnp.pad(velocity, ((0, 0), (1, 1), (0, 0), (0, 0)))
    blocks = math.gcd(depth, 8)
    offsets = jnp.arange(depth // blocks, dtype=jnp.int32) * blocks

    def advance(offset):
        window = lax.dynamic_slice_in_dim(padded, offset, blocks + 2, 1)
        middle = window[:, 1:-1]
        return tendency(middle, jnp.roll(middle, -1, 3), jnp.roll(middle, 1, 3), jnp.roll(middle, -1, 2), jnp.roll(middle, 1, 2), window[:, 2:], window[:, :-2])
    stacked = lax.map(advance, offsets)
    return jnp.moveaxis(stacked, 0, 1).reshape(velocity.shape)

def dct_tables(count):
    integer_ids = jnp.arange(count, dtype=jnp.int32)
    phases = integer_ids[:, None] * (2 * integer_ids[None, :] + 1) % (4 * count)
    forward = jnp.cos(jnp.pi * phases.astype(jnp.float32) / (2 * count))
    weights = jnp.where(integer_ids == 0, 1.0, 2.0).astype(jnp.float32) / count
    inverse = forward.T * weights[None, :]
    return (forward, inverse)

def eigen(wavenum, length):
    sine_val = jnp.sin(jnp.pi * wavenum.astype(jnp.float32) / length)
    return 4.0 * sine_val * sine_val

def project(star, width):
    east_vel, north_vel, upward_vel = (star[0], star[1], star[2])
    low_up = jnp.concatenate([jnp.zeros_like(upward_vel[:1]), upward_vel[:-1]], 0)
    divergence = east_vel - jnp.roll(east_vel, 1, 2) + (north_vel - jnp.roll(north_vel, 1, 1)) + (upward_vel - low_up)
    forward, inverse = dct_tables(NZ)
    levels = jnp.einsum('mz,zyx->myx', forward, divergence, precision=lax.Precision.HIGHEST)
    spectrum = jnp.fft.rfft2(levels, axes=(1, 2))
    wave_z = jnp.arange(NZ, dtype=jnp.int32)
    wave_y = jnp.arange(NY, dtype=jnp.int32)
    wave_x = jnp.arange(width // 2 + 1, dtype=jnp.int32)
    summed = eigen(wave_z, 2 * NZ)[:, None, None] + eigen(wave_y, NY)[None, :, None] + eigen(wave_x, width)[None, None, :]
    null_mode = (wave_z[:, None, None] == 0) & (wave_y[None, :, None] == 0) & (wave_x[None, None, :] == 0)
    spectrum = jnp.where(null_mode, 0.0, -spectrum / jnp.where(null_mode, 1.0, summed))
    levels = jnp.fft.irfft2(spectrum, s=(NY, width), axes=(1, 2))
    pressure = jnp.einsum('zm,myx->zyx', inverse, levels, precision=lax.Precision.HIGHEST)
    step_x = jnp.roll(pressure, -1, 2) - pressure
    step_y = jnp.roll(pressure, -1, 1) - pressure
    step_z = jnp.concatenate([pressure[1:] - pressure[:-1], jnp.zeros_like(pressure[:1])], 0)
    return star - jnp.stack([step_x, step_y, step_z])

def reference(vel_pre, vel_farm, thrust, turbine_cells, inflow_rows):
    star_pre = predict_domain(vel_pre)
    star_farm = predict_domain(vel_farm)
    cell_z, cell_y, cell_x = (turbine_cells[0], turbine_cells[1], turbine_cells[2])
    stream_vel = vel_farm[0, cell_z, cell_y, cell_x]
    thrust_force = -time_step * thrust[:, None] * jnp.abs(stream_vel) * stream_vel
    star_farm = star_farm.at[0, cell_z, cell_y, cell_x].add(thrust_force)
    inflow = vel_pre[:, :, :, NXP - 1][:, :, inflow_rows]
    weight = jnp.maximum(FRINGE - jnp.arange(NXF, dtype=jnp.int32), 0).astype(jnp.float32) / FRINGE
    star_farm = star_farm + weight * (inflow[..., None] - star_farm)
    star_pre = star_pre.at[2, NZ - 1].set(0.0)
    star_farm = star_farm.at[2, NZ - 1].set(0.0)
    return (project(star_pre, NXP), project(star_farm, NXF))
```

```python
import functools

import jax
import jax.numpy as jnp
from jax import lax
from jax.experimental import pallas as pl
from jax.experimental.pallas import tpu as pltpu
from jax.sharding import PartitionSpec as P

FRINGE = 32


time_step = 0.1
viscosity = 0.05
smagorinsky = 0.03
highest = lax.Precision.HIGHEST


def shifted(block, axis, distance):
    devices = range(lax.axis_size(axis))
    route = [((i - distance) % len(devices), i) for i in devices]
    return lax.ppermute(block, axis, route)


def shifted_2(value, axis, steps):
    count = lax.axis_size(axis)
    first, last = (max(0, -steps), min(count, count - steps))
    return lax.ppermute(value, axis, [(source, source + steps) for source in range(first, last)])


def tendency(velocity, up_x, dn_x, up_y, dn_y, up_z, dn_z):
    grad_x = 0.5 * (up_x - dn_x)
    grad_y = 0.5 * (up_y - dn_y)
    grad_z = 0.5 * (up_z - dn_z)
    laplace = up_x + dn_x + up_y + dn_y + up_z + dn_z - 6.0 * velocity
    advect = velocity[0:1] * grad_x + velocity[1:2] * grad_y + velocity[2:3] * grad_z
    shear_sq = 2.0 * (grad_x[0] * grad_x[0] + grad_y[1] * grad_y[1] + grad_z[2] * grad_z[2])
    shear_sq = shear_sq + (grad_y[0] + grad_x[1]) * (grad_y[0] + grad_x[1])
    shear_sq = shear_sq + (grad_z[0] + grad_x[2]) * (grad_z[0] + grad_x[2])
    shear_sq = shear_sq + (grad_z[1] + grad_y[2]) * (grad_z[1] + grad_y[2])
    eddy_visc = viscosity + smagorinsky * jnp.sqrt(shear_sq)
    return velocity + time_step * (eddy_visc * laplace - advect)


def span_neighbor(planes, offset):
    return shifted(planes, "gy", offset)


def vertical_neighbor(planes, offset):
    return shifted_2(planes, "gz", offset)


def eigen(wavenum, length):
    sine_val = jnp.sin(jnp.pi * wavenum.astype(jnp.float32) / length)
    return 4.0 * sine_val * sine_val


def dct_tables(count):
    integer_ids = jnp.arange(count, dtype=jnp.int32)
    phases = integer_ids[:, None] * (2 * integer_ids[None, :] + 1) % (4 * count)
    forward = jnp.cos(jnp.pi * phases.astype(jnp.float32) / (2 * count))
    weights = jnp.where(integer_ids == 0, 1.0, 2.0).astype(jnp.float32) / count
    inverse = forward.T * weights[None, :]
    return (forward, inverse)


def hartley(count):
    ids = jnp.arange(count, dtype=jnp.int32)
    angles = 2.0 * jnp.pi * (ids[:, None] * ids[None, :] % count).astype(jnp.float32) / count
    return jnp.cos(angles) + jnp.sin(angles)


def sine_table(span):
    ids = jnp.arange(span, dtype=jnp.int32)
    phases = ids[:, None] * ids[None, :] % (2 * span)
    table = jnp.sqrt(2.0 / span) * jnp.sin(jnp.pi * phases.astype(jnp.float32) / span)
    return table.at[0, 0].set(1.0)


def mm(a, b, dims=(((1,), (0,)), ((), ()))):
    return lax.dot_general(a, b, dims, precision=highest, preferred_element_type=jnp.float32)


def forward_kernel(block, rate_ref, r_ref, dct_ref, dst_ref, base_ref, edge_ref, g_ref, e_ref):
    first = pl.program_id(0) * block
    parts, _, depth, span = r_ref.shape
    lane = lax.broadcasted_iota(jnp.int32, base_ref.shape, 1)

    def step(k, carry):
        column = r_ref[:, k].reshape(parts * depth, span)
        modal = mm(mm(dct_ref[...], column), dst_ref[...])
        scale = jnp.where(lane == 0, 1.0, base_ref[...] + rate_ref[first + k])
        solved = -modal / scale
        g_ref[k] = solved
        e_ref[k] = mm(edge_ref[...], solved, (((1,), (1,)), ((), ())))
        return carry

    lax.fori_loop(0, block, step, 0)


def backward_kernel(block, rate_ref, g_ref, p_ref, dct_ref, dst_ref, base_ref, edge_ref, o_ref):
    first = pl.program_id(0) * block
    parts, _, depth, span = o_ref.shape
    lane = lax.broadcasted_iota(jnp.int32, base_ref.shape, 1)

    def step(k, carry):
        border = mm(p_ref[k], edge_ref[...], (((0,), (0,)), ((), ())))
        scale = base_ref[...] + rate_ref[first + k]
        modal = jnp.where(lane == 0, border, g_ref[k] + border / scale)
        column = mm(dct_ref[...], mm(modal, dst_ref[...]))
        o_ref[:, k] = column.reshape(parts, depth, span)
        return carry

    lax.fori_loop(0, block, step, 0)


def solve_pressure(spectral, rate_x, count_z, count_y, zone_y, total_z):
    modes, depth, span = spectral.shape
    per = modes // count_z
    block = 8
    whole = lax.all_to_all(spectral, "gz", split_axis=0, concat_axis=0, tiled=True)
    whole = whole.reshape(count_z, per, depth, span)
    dct_fwd, dct_inv = dct_tables(total_z)
    dst = sine_table(span)
    ids = jnp.arange(span, dtype=jnp.int32)
    rate_z = eigen(jnp.arange(total_z, dtype=jnp.int32), 2 * total_z)
    rate_y = jnp.where(ids == 0, 1.0, eigen(ids, 2 * span))
    base = rate_z[:, None] + rate_y[None, :]
    tail = dst[span - 1]
    lead = jnp.where(ids == 0, 1.0, dst[1])
    edge = jnp.zeros((8, span), jnp.float32).at[0].set(lead).at[1].set(tail)
    full = lambda *shape: pl.BlockSpec(shape, lambda i: (0,) * len(shape))
    smem = pl.BlockSpec(memory_space=pltpu.SMEM)
    columns = pl.BlockSpec((count_z, block, depth, span), lambda i: (0, i, 0, 0))
    modal = pl.BlockSpec((block, total_z, span), lambda i: (i, 0, 0))
    pairs = pl.BlockSpec((block, 8, total_z), lambda i: (i, 0, 0))
    params = pltpu.CompilerParams(vmem_limit_bytes=48 << 20)
    solved, ends = pl.pallas_call(
        functools.partial(forward_kernel, block),
        grid=(per // block,),
        in_specs=[smem, columns, full(total_z, total_z), full(span, span), full(total_z, span), full(8, span)],
        out_specs=[modal, pairs],
        out_shape=[
            jax.ShapeDtypeStruct((per, total_z, span), jnp.float32),
            jax.ShapeDtypeStruct((per, 8, total_z), jnp.float32),
        ],
        compiler_params=params,
        name="solve_forward",
    )(rate_x, whole, dct_fwd, dst, base, edge)
    sent = jnp.concatenate([ends[:, 0], ends[:, 1]], 0)
    every = lax.all_gather(sent, "gy", axis=0)
    given = every[:, :per] + jnp.roll(every[:, per:], 1, 0)
    cas = hartley(count_y)
    rate = rate_x[:, None] + rate_z[None, :]
    null = rate == 0.0
    safe = jnp.where(null, 1.0, rate)
    half = 0.5 * jnp.sqrt(safe)
    root = jnp.sqrt(1.0 + half * half)
    theta = 2.0 * jnp.log1p(half + half * half / (1.0 + root))
    decay = jnp.exp(-span * theta)
    lift = -jnp.expm1(-span * theta)
    turn = 0.5 * eigen(jnp.arange(count_y, dtype=jnp.int32), count_y)[:, None, None]
    factor = (4.0 * half * root) / (lift * (1.0 + decay))
    symbol = factor * (lift * lift + 2.0 * decay * turn)
    symbol = jnp.where(null, 2.0 * turn / span, symbol)
    drop = symbol == 0.0
    inner = jnp.einsum("kj,jxm->kxm", cas, given, precision=highest)
    inner = jnp.where(drop, 0.0, inner / jnp.where(drop, 1.0, symbol)) / count_y
    own = jnp.stack([zone_y, (zone_y + 1) % count_y])
    rows = jnp.sum(jnp.where(own[:, None, None] == jnp.arange(count_y)[None, :, None], cas[None], 0.0), 1)
    borders = jnp.einsum("ik,kxm->xim", rows, inner, precision=highest)
    borders = jnp.concatenate([borders, jnp.zeros((per, 6, total_z), jnp.float32)], 1)
    back = pl.pallas_call(
        functools.partial(backward_kernel, block),
        grid=(per // block,),
        in_specs=[smem, modal, pairs, full(total_z, total_z), full(span, span), full(total_z, span), full(8, span)],
        out_specs=columns,
        out_shape=jax.ShapeDtypeStruct((count_z, per, depth, span), jnp.float32),
        compiler_params=params,
        name="solve_backward",
    )(rate_x, solved, borders, dct_inv, dst, base, edge)
    back = back.reshape(modes, depth, span)
    return lax.all_to_all(back, "gz", split_axis=0, concat_axis=0, tiled=True)


def body(vel_pre, vel_farm, thrust, turbine_cells, inflow_rows):
    count_z = lax.axis_size("gz")
    count_y = lax.axis_size("gy")
    zone_z = lax.axis_index("gz")
    zone_y = lax.axis_index("gy")
    depth = vel_pre.shape[1]
    span = vel_pre.shape[2]
    len_pre = vel_pre.shape[3]
    len_farm = vel_farm.shape[3]
    total_z = depth * count_z
    total_y = span * count_y
    modes = len_pre + len_farm
    low_y = span_neighbor(jnp.concatenate([vel_pre[:, :, -1:], vel_farm[:, :, -1:]], -1), 1)
    high_y = span_neighbor(jnp.concatenate([vel_pre[:, :, :1], vel_farm[:, :, :1]], -1), -1)
    low_z = vertical_neighbor(jnp.concatenate([vel_pre[:, -1:], vel_farm[:, -1:]], -1), 1)
    high_z = vertical_neighbor(jnp.concatenate([vel_pre[:, :1], vel_farm[:, :1]], -1), -1)

    def predict(velocity, first_col, last_col):
        up_y = jnp.concatenate([velocity[:, :, 1:], high_y[..., first_col:last_col]], 2)
        dn_y = jnp.concatenate([low_y[..., first_col:last_col], velocity[:, :, :-1]], 2)
        up_z = jnp.concatenate([velocity[:, 1:], high_z[..., first_col:last_col]], 1)
        dn_z = jnp.concatenate([low_z[..., first_col:last_col], velocity[:, :-1]], 1)
        return tendency(
            velocity, jnp.roll(velocity, -1, 3), jnp.roll(velocity, 1, 3), up_y, dn_y, up_z, dn_z
        )

    star_pre = predict(vel_pre, 0, len_pre)
    star_farm = predict(vel_farm, len_pre, modes)
    cell_z = turbine_cells[0] - zone_z * depth
    cell_y = turbine_cells[1] - zone_y * span
    cell_x = turbine_cells[2]
    inside = (cell_z >= 0) & (cell_z < depth) & (cell_y >= 0) & (cell_y < span)
    flat_cell = jnp.where(inside, (cell_z * span + cell_y) * len_farm + cell_x, 0).reshape(-1)
    stream_vel = vel_farm[0].reshape(-1)[flat_cell].reshape(inside.shape)
    thrust_force = jnp.where(
        inside, -time_step * thrust[:, None] * jnp.abs(stream_vel) * stream_vel, 0.0
    )
    stream_new = (
        star_farm[0]
        .reshape(-1)
        .at[flat_cell]
        .add(thrust_force.reshape(-1))
        .reshape(depth, span, len_farm)
    )
    star_farm = jnp.concatenate([stream_new[None], star_farm[1:]], 0)
    outlet = vel_pre[:, :, :, -1].reshape(3 * depth, span)
    whole_plane = lax.all_gather(outlet, "gy", axis=0)
    chosen = (
        inflow_rows[None, :, None]
        == jnp.arange(total_y, dtype=jnp.int32).reshape(count_y, 1, span)
    ).astype(jnp.float32)
    inflow = jnp.einsum("gcs,gys->cy", whole_plane, chosen, precision=highest).reshape(3, depth, span)
    weight = (
        jnp.maximum(FRINGE - jnp.arange(len_farm, dtype=jnp.int32), 0).astype(jnp.float32) / FRINGE
    )
    star_farm = star_farm + weight * (inflow[..., None] - star_farm)
    z_global = zone_z * depth + jnp.arange(depth, dtype=jnp.int32)
    below_top = (z_global < total_z - 1).astype(jnp.float32)
    lid_mask = jnp.stack([jnp.ones_like(below_top), jnp.ones_like(below_top), below_top])[
        :, :, None, None
    ]
    star_pre = star_pre * lid_mask
    star_farm = star_farm * lid_mask
    low_north = span_neighbor(jnp.concatenate([star_pre[1, :, -1:], star_farm[1, :, -1:]], -1), 1)
    low_up = vertical_neighbor(jnp.concatenate([star_pre[2, -1:], star_farm[2, -1:]], -1), 1)

    def divergence_of(star, first_col, last_col):
        east_vel, north_vel, upward_vel = (star[0], star[1], star[2])
        dn_north = jnp.concatenate([low_north[..., first_col:last_col], north_vel[:, :-1]], 1)
        dn_up = jnp.concatenate([low_up[..., first_col:last_col], upward_vel[:-1]], 0)
        return east_vel - jnp.roll(east_vel, 1, 2) + (north_vel - dn_north) + (upward_vel - dn_up)

    cas_pre = hartley(len_pre)
    cas_farm = hartley(len_farm)
    spectral = jnp.concatenate(
        [
            jnp.einsum("mx,zyx->mzy", cas_pre, divergence_of(star_pre, 0, len_pre), precision=highest),
            jnp.einsum("mx,zyx->mzy", cas_farm, divergence_of(star_farm, len_pre, modes), precision=highest),
        ],
        0,
    )
    kx_modes = zone_z * (modes // count_z) + jnp.arange(modes // count_z, dtype=jnp.int32)
    rate_x = jnp.where(
        kx_modes < len_pre, eigen(kx_modes, len_pre), eigen(kx_modes - len_pre, len_farm)
    )
    solved = solve_pressure(spectral, rate_x, count_z, count_y, zone_y, total_z)
    pressure = jnp.concatenate(
        [
            jnp.einsum("mzy,mx->zyx", solved[:len_pre], cas_pre / len_pre, precision=highest),
            jnp.einsum("mzy,mx->zyx", solved[len_pre:], cas_farm / len_farm, precision=highest),
        ],
        -1,
    )
    high_north = span_neighbor(pressure[:, :1], -1)
    high_up = vertical_neighbor(pressure[:1], -1)

    def correct(star, first_col, last_col):
        press_part = pressure[..., first_col:last_col]
        step_x = jnp.roll(press_part, -1, 2) - press_part
        step_y = (
            jnp.concatenate([press_part[:, 1:], high_north[..., first_col:last_col]], 1)
            - press_part
        )
        step_z = (
            jnp.concatenate([press_part[1:], high_up[..., first_col:last_col]], 0) - press_part
        ) * below_top[:, None, None]
        return star - jnp.stack([step_x, step_y, step_z])

    return (correct(star_pre, 0, len_pre), correct(star_farm, len_pre, modes))


def solution(mesh):
    in_specs = (P(None, "gz", "gy", None), P(None, "gz", "gy", None), P(), P(), P("gy"))
    out_specs = (P(None, "gz", "gy", None), P(None, "gz", "gy", None))
    return jax.shard_map(body, mesh=mesh, in_specs=in_specs, out_specs=out_specs, check_vma=False)
```
